512 devices in a mesh: tile: 64 (over z, x, core), row: 8 (over y).
Axes of the slice: x: 4, y: 8, z: 8, core: 2. Of those that a mesh axis runs over, the one named last changes fastest.
Arguments:
- swath_blocks: bfloat16 [64, 8, 768, 2048], P('tile', 'row'), may hold values from -6 to 6
- footprint: int32 [64, 8, 768, 1], P('tile', 'row'), may hold values from 0 to 511; in each aligned block of 768 rows (0 to 767, 768 to 1535, ..., all dimensions but the last counted through in order) at most 2 rows name the same one
- cell_row: int32 [64, 8, 768], P('tile', 'row'), may hold values from 0 to 127
- tile_pick: int32 [64, 8, 768], P('tile', 'row'), may hold values from 0 to 3
- sensor: int32 [64, 8, 768], P('tile', 'row'), may hold values from 0 to 1
- bandpass_offset: float32 [2, 8, 8], replicated, may hold values from -0.4 to 0.4
- weight_tiles: bfloat16 [4, 256, 256], replicated, may hold values from -0.375 to 0.375
- lookup_table: float32 [8, 33], replicated, may hold values from 0.5 to 2
- lookup_bin: int32 [64, 1024, 256], P('tile', 'row'), may hold values from 0 to 31
- lookup_frac: float32 [64, 1024, 256], P('tile', 'row'), may hold values from 0 to 1
- brdf_params: float32 [8, 3], replicated, may hold values from 0.05 to 1
- vol_kernel: float32 [64, 1024, 256], P('tile', 'row'), may hold values from 0.1 to 2
- geo_kernel: float32 [64, 1024, 256], P('tile', 'row'), may hold values from 0.1 to 2
- clear_mask: int32 [64, 1024, 256], P('tile', 'row'), may hold values 0 or 1
Outputs:
- nbar: bfloat16 [64, 1024, 2048], P('tile', 'row')
The draws below stay inside these ranges and needn't reach their ends.
Inputs may be any that keep to these rules, and one draw needn't show every extreme that they name: `footprint`: at most 2 of the blocks of one device name one destination, and in every draw some destination is named by exactly 2 of them.
All inputs are finite; a program needn't handle non-finite values. No bound on the sum of `clear_mask` on one device may be relied on, other than what follows from the above.
Results may differ from the reference program's by a relative error of at most 0.0057.
Values may be sent and summed in bfloat16 or wider, within the bound.
A program may use at most 64 MiB of HBM per device.

```python
import math
import jax
import jax.numpy as jnp
import numpy as np
from jax import lax

BANDS = 8
BPIX = 256
KT = 4
NBIN = 32
SB = 768
NCB = 128
DESTS = 512
CAP = 2
GR = 1024
N_TILE = 64
N_ROW = 8


def with_ends(array, rng, least, top_value):
    shape = array.shape
    place = [jax.random.randint(jax.random.fold_in(rng, axis), (), 0, shape[axis]) for axis in range(len(shape))]
    array = array.at[tuple(place)].set(least)
    longest = shape.index(max(shape))
    place[longest] = (place[longest] + 1) % shape[longest]
    return array.at[tuple(place)].set(top_value)


def block_levels(own_key, shape, cuts, smallest, largest):
    factor_of, own = 1.0, jax.random.fold_in(own_key, 6)
    for axis_at, parts in cuts:
        steps = jnp.exp(jax.random.uniform(jax.random.fold_in(own, axis_at), (parts,), jnp.float32, smallest / len(cuts), largest / len(cuts)))
        factor_of = factor_of * jnp.repeat(steps, shape[axis_at] // parts).reshape([-1 if axis == axis_at else 1 for axis in range(len(shape))])
    return factor_of


def routed_block(rng, own, number, rows, amount, top, limit, slope):
    order = jax.random.permutation(rng, amount)
    crowded, ordinary = load_shares(amount, rows * top, limit, slope, True), load_shares(amount, rows * top, limit, slope, False)
    places = jnp.arange(amount)

    def named(lengths, turn):
        used = int((lengths > 0).sum())
        fixed = max(1, used // 4)
        passed = fixed + (places - fixed + turn * (used - fixed)) % max(1, amount - fixed)
        return jnp.zeros((amount,), jnp.int32).at[order[jnp.where(places < fixed, places, passed)]].set(jnp.asarray(lengths, jnp.int32))

    lengths = jnp.where(number % 4 == 0, named(crowded, number // 4), named(ordinary, number - number // 4 - 1))
    mixed = jax.random.permutation(jax.random.fold_in(own, 3), amount)
    giver, taker = mixed[0:amount // 2 * 2:2], mixed[1:amount // 2 * 2:2]
    room = jnp.minimum(lengths[giver] - 1, limit - lengths[taker]) // 2
    room = jnp.where((giver == order[0]) | (taker == order[0]) | (lengths[taker] == 0), 0, jnp.maximum(room, 0))
    passed = jax.random.randint(jax.random.fold_in(own, 4), (amount // 2,), 0, 1 << 20) % (room + 1)
    lengths = lengths.at[giver].add(-passed).at[taker].add(passed)
    labels = jnp.searchsorted(jnp.cumsum(lengths), jnp.arange(rows * top), side="right").astype(jnp.int32)
    listing = labels.reshape(top, rows).T
    listing = listing[jax.random.permutation(jax.random.fold_in(own, 1), rows)]
    turn = jax.random.randint(jax.random.fold_in(own, 2), (rows, 1), 0, top)
    return jnp.take_along_axis(listing, (jnp.arange(top)[None, :] + turn) % top, axis=1)


def load_shares(amount, total, bound, lean, full):
    portions = [(1 << 20) // math.isqrt(rank ** lean) + 1 for rank in range(1, amount + 1)]
    largest = bound if full else min(bound, max(-(-total // amount), total * portions[0] // sum(portions)))
    least = 1 if total - largest >= amount - 1 else 0
    counts, rest = [largest] + [least] * (amount - 1), total - largest - least * (amount - 1)
    while rest > 0:
        movable = [i for i in range(1, amount) if counts[i] < largest] or [i for i in range(1, amount) if counts[i] < bound]
        whole, left = sum([portions[i] for i in movable]), rest
        for i in movable:
            extra = min(bound - counts[i], max(1, left * portions[i] // whole), rest)
            counts[i] = counts[i] + extra
            rest = rest - extra
    return np.array(counts)


def bell_draw(stream_key, dims, deviation, reach, shards=(), kind=jnp.bfloat16):
    array = deviation * jax.random.normal(stream_key, dims, jnp.float32)
    if shards:
        array = array * block_levels(stream_key, dims, shards, -0.22, 0.18)
    return jnp.clip(array, -reach, reach).astype(kind)


def setup_inputs(seed: int = 0) -> dict:
    arg_keys = jax.random.split(jax.random.key(seed), 15)
    swath_blocks = bell_draw(arg_keys[0], (N_TILE, N_ROW, SB, BANDS * BPIX), 1.0, 6.0, ((0, 64), (1, 8)))
    footprint_keys = jax.random.split(jax.random.fold_in(arg_keys[1], 1), N_TILE * N_ROW * SB // SB)
    footprint_turns = jax.random.permutation(jax.random.fold_in(arg_keys[1], 3), N_TILE * N_ROW * SB // SB)
    footprint = jax.vmap(lambda own, number: routed_block(jax.random.fold_in(arg_keys[1], 2), own, number, SB, DESTS, 1, CAP, 2))(footprint_keys, footprint_turns).reshape((N_TILE, N_ROW, SB, 1))
    cell_row = with_ends(jax.random.randint(arg_keys[2], (N_TILE, N_ROW, SB), 0, NCB), jax.random.fold_in(arg_keys[2], 1), 0, NCB - 1).astype(jnp.int32)
    tile_pick = with_ends(jax.random.randint(arg_keys[3], (N_TILE, N_ROW, SB), 0, KT), jax.random.fold_in(arg_keys[3], 1), 0, KT - 1).astype(jnp.int32)
    sensor = with_ends(jax.random.randint(arg_keys[4], (N_TILE, N_ROW, SB), 0, 2), jax.random.fold_in(arg_keys[4], 1), 0, 1).astype(jnp.int32)
    bandpass_offset = jnp.clip(jax.random.uniform(arg_keys[5], (2, BANDS, BANDS), jnp.float32, -0.4, 0.4), -0.4, 0.4)
    weight_tiles = bell_draw(arg_keys[6], (KT, BPIX, BPIX), BPIX ** -0.5, 0.375)
    lookup_table = jnp.clip(jnp.exp(jax.random.uniform(arg_keys[7], (BANDS, NBIN + 1), jnp.float32, math.log(0.5), math.log(2.0))), 0.5, 2.0)
    lookup_bin = with_ends(jax.random.randint(arg_keys[8], (N_TILE, GR, BPIX), 0, NBIN), jax.random.fold_in(arg_keys[8], 1), 0, NBIN - 1).astype(jnp.int32)
    lookup_frac = jnp.clip(1.0 * jax.random.uniform(arg_keys[9], (N_TILE, GR, BPIX), jnp.float32) ** block_levels(arg_keys[9], (N_TILE, GR, BPIX), ((0, 64), (1, 8)), -0.2, 0.2), 0.0, 1.0)
    brdf_params = jnp.clip(jnp.exp(jax.random.uniform(arg_keys[10], (BANDS, 3), jnp.float32, math.log(0.05), math.log(1.0))), 0.05, 1.0)
    vol_kernel = jnp.clip(jnp.exp(math.log(2.0) - 2.9957323 * jax.random.uniform(arg_keys[11], (N_TILE, GR, BPIX), jnp.float32) ** block_levels(arg_keys[11], (N_TILE, GR, BPIX), ((0, 64), (1, 8)), -0.2, 0.2)), 0.1, 2.0)
    geo_kernel = jnp.clip(jnp.exp(math.log(2.0) - 2.9957323 * jax.random.uniform(arg_keys[12], (N_TILE, GR, BPIX), jnp.float32) ** block_levels(arg_keys[12], (N_TILE, GR, BPIX), ((0, 64), (1, 8)), -0.2, 0.2)), 0.1, 2.0)
    clear_mask = with_ends((jax.random.randint(arg_keys[13], (N_TILE, GR, BPIX), 0, 5) < 4).astype(jnp.int32), jax.random.fold_in(arg_keys[13], 1), 0, 1)
    return dict(swath_blocks=swath_blocks, footprint=footprint, cell_row=cell_row, tile_pick=tile_pick, sensor=sensor, bandpass_offset=bandpass_offset, weight_tiles=weight_tiles, lookup_table=lookup_table, lookup_bin=lookup_bin, lookup_frac=lookup_frac, brdf_params=brdf_params, vol_kernel=vol_kernel, geo_kernel=geo_kernel, clear_mask=clear_mask)


nadir_volume = 0.3
nadir_geometric = 0.6


def reference(swath_blocks, footprint, cell_row, tile_pick, sensor, bandpass_offset, weight_tiles, lookup_table, lookup_bin, lookup_frac, brdf_params, vol_kernel, geo_kernel, clear_mask):
    row_width = BANDS * BPIX
    mixing = jnp.eye(BANDS, dtype=jnp.float32)[None, :, :] + bandpass_offset
    stacked_weights = weight_tiles.reshape(KT * BPIX, BPIX)
    device_count = N_TILE * N_ROW
    xs = (swath_blocks.reshape(device_count, SB, row_width),
          footprint.reshape(device_count, SB),
          cell_row.reshape(device_count, SB),
          tile_pick.reshape(device_count, SB),
          sensor.reshape(device_count, SB))

    def add_group(accum_grid, operands):
        payload, target, rows_here, picks, sensors = operands
        chosen_mix = mixing[sensors]
        banded = jnp.einsum('sbc,scp->sbp', chosen_mix, payload.reshape(SB, BANDS, BPIX).astype(jnp.float32), precision=lax.Precision.HIGHEST).astype(jnp.bfloat16)
        chosen = picks[:, None] == jnp.arange(KT, dtype=jnp.int32)[None, :]
        spread = jnp.where(chosen[:, None, :, None], banded[:, :, None, :], jnp.zeros((), jnp.bfloat16))
        resampled = jnp.dot(spread.reshape(SB * BANDS, KT * BPIX), stacked_weights, preferred_element_type=jnp.float32).astype(jnp.bfloat16)
        tile_index = target // N_ROW
        grid_row = (target % N_ROW) * NCB + rows_here
        accum_grid = accum_grid.at[tile_index, grid_row].add(resampled.reshape(SB, row_width).astype(jnp.float32))
        return accum_grid, None

    accum_grid = jnp.zeros((N_TILE, GR, row_width), jnp.float32)
    accum_grid, unused = lax.scan(add_group, accum_grid, xs)
    padded = jnp.pad(accum_grid, ((0, 0), (1, 1), (0, 0)))
    smoothed = 0.25 * padded[:, :-2] + 0.5 * padded[:, 1:-1] + 0.25 * padded[:, 2:]
    smoothed = smoothed.reshape(N_TILE, GR, BANDS, BPIX)
    lower_value = jnp.moveaxis(lookup_table[:, lookup_bin], 0, 2)
    upper_value = jnp.moveaxis(lookup_table[:, lookup_bin + 1], 0, 2)
    fraction = lookup_frac[:, :, None, :]
    table_value = lower_value * (1.0 - fraction) + upper_value * fraction
    isotropic = brdf_params[:, 0][None, None, :, None]
    volume = brdf_params[:, 1][None, None, :, None]
    geometric = brdf_params[:, 2][None, None, :, None]
    numerator = isotropic + volume * nadir_volume + geometric * nadir_geometric
    denominator = isotropic + volume * vol_kernel[:, :, None, :] + geometric * geo_kernel[:, :, None, :]
    cfactor = numerator / denominator
    result = smoothed * table_value * cfactor * clear_mask[:, :, None, :].astype(jnp.float32)
    return result.reshape(N_TILE, GR, row_width).astype(jnp.bfloat16)
```

```python
import functools

import jax
import jax.numpy as jnp
from jax import lax
from jax.experimental import pallas as pl
from jax.experimental.pallas import tpu as pltpu
from jax.sharding import PartitionSpec as P

nadir_volume = 0.3
nadir_geometric = 0.6
MESH = pl.DeviceIdType.MESH
CHUNKS = 4
HALF = 128


def offsets(t):
    spread = (t // 64 + t) % 8
    return t % 8, (t // 8 + t) % 8, spread // 2, spread % 2


def slot_of(target, rank, group):
    tile = lax.axis_index("tile")
    row = lax.axis_index("row")
    to_tile, to_row = target // 8, target % 8
    dy = (to_row - row) % 8
    dz = (to_tile // 8 - tile // 8) % 8
    dx = ((to_tile // 2) % 4 - (tile // 2) % 4) % 4
    dc = (to_tile % 2 - tile % 2) % 2
    t = ((dx * 2 + dc - dy) % 8) * 64 + ((dz - dy) % 8) * 8 + dy
    return ((t // group) * 2 + rank) * group + t % group


def kernel(
    mixing_ref,
    table_ref,
    brdf_ref,
    blocks_ref,
    position_ref,
    code_ref,
    weights_ref,
    bin_ref,
    frac_ref,
    vol_ref,
    geo_ref,
    mask_ref,
    out_ref,
    outgoing,
    incoming,
    tags_out,
    tags_in,
    unpacked,
    sums,
    resampled,
    grid,
    factor,
    edge_out,
    edge_in,
    send_sem,
    recv_sem,
    tag_send_sem,
    tag_recv_sem,
    edge_send_sem,
    edge_recv_sem,
):
    devices = outgoing.shape[0]
    blocks = blocks_ref.shape[0]
    bands = 8
    pixels = 256
    cells = out_ref.shape[0]
    group = devices // CHUNKS
    tile = lax.axis_index("tile")
    row = lax.axis_index("row")
    z, x, core = tile // 8, (tile // 2) % 4, tile % 2

    lane = lax.broadcasted_iota(jnp.int32, (group, 128), 1)
    for k in range(CHUNKS):
        slot_number = lax.broadcasted_iota(jnp.int32, (2 * group, blocks), 0) + k * 2 * group
        holds = position_ref[...] == slot_number
        code = jnp.sum(jnp.where(holds, code_ref[...] + 1, 0), axis=1, keepdims=True) - 1
        tags_out[pl.ds(k * group, group)] = jnp.where(
            lane == 0, code[:group], code[group:]
        ).reshape(group, 1, 128)
        chosen = holds.astype(jnp.bfloat16)
        for b in range(bands):
            moved = jnp.dot(
                chosen, blocks_ref[:, pl.ds(b * pixels, pixels)], preferred_element_type=jnp.float32
            )
            for slot in range(2):
                for h in range(pixels // HALF):
                    unpacked[
                        pl.ds((h * group * 2 + slot) * bands + b, group, stride=2 * bands), :
                    ] = moved[slot * group : (slot + 1) * group, h * HALF : (h + 1) * HALF]
        for i in range(group // 32):
            halves = [
                unpacked[pl.ds((h * group + i * 32) * 2 * bands, 512), :]
                for h in range(pixels // HALF)
            ]
            outgoing[pl.ds(k * group + i * 32, 32)] = (
                jnp.concatenate(halves, axis=1).astype(jnp.bfloat16).reshape(32, 2 * bands, pixels)
            )
        if k == 0:
            incoming[0] = outgoing[0]
            tags_in[0] = tags_out[0]

        @pl.loop(max(1, k * group), (k + 1) * group)
        def _(t):
            dy, dz, dx, dc = offsets(t)
            to_tile = ((z + dz) % 8) * 8 + ((x + dx) % 4) * 2 + (core + dc) % 2
            to_row = (row + dy) % 8
            pltpu.make_async_remote_copy(
                src_ref=outgoing.at[t],
                dst_ref=incoming.at[t],
                send_sem=send_sem,
                recv_sem=recv_sem.at[k],
                device_id=(to_tile, to_row),
                device_id_type=MESH,
            ).start()
            pltpu.make_async_remote_copy(
                src_ref=tags_out.at[t],
                dst_ref=tags_in.at[t],
                send_sem=tag_send_sem,
                recv_sem=tag_recv_sem.at[k],
                device_id=(to_tile, to_row),
                device_id_type=MESH,
            ).start()

    bins = table_ref.shape[1] - 1

    @pl.loop(0, cells // 8)
    def _(g):
        rows = pl.ds(pl.multiple_of(g * 8, 8), 8)
        which = bin_ref[rows, :]
        part = frac_ref[rows, :]
        volume_angle = vol_ref[rows, :]
        geometric_angle = geo_ref[rows, :]
        keep = mask_ref[rows, :].astype(jnp.float32)
        lower = [jnp.full((8, pixels), table_ref[b, 0]) for b in range(bands)]
        upper = [jnp.full((8, pixels), table_ref[b, 1]) for b in range(bands)]
        for n in range(1, bins):
            here = which == n
            for b in range(bands):
                lower[b] = jnp.where(here, table_ref[b, n], lower[b])
                upper[b] = jnp.where(here, table_ref[b, n + 1], upper[b])
        for b in range(bands):
            value = lower[b] * (1.0 - part) + upper[b] * part
            isotropic, volume, geometric = brdf_ref[b, 0], brdf_ref[b, 1], brdf_ref[b, 2]
            numerator = isotropic + volume * nadir_volume + geometric * nadir_geometric
            denominator = isotropic + volume * volume_angle + geometric * geometric_angle
            factor[rows, pl.ds(b * pixels, pixels)] = value * (numerator / denominator) * keep

    codes = sums.shape[0]
    for k in range(CHUNKS):
        low = max(1, k * group)
        part = pl.ds(low, (k + 1) * group - low)
        pltpu.make_async_copy(tags_in.at[part], tags_in.at[part], tag_recv_sem.at[k]).wait()
        pltpu.make_async_copy(incoming.at[part], incoming.at[part], recv_sem.at[k]).wait()
        for i in range(group // 32):
            arrived = incoming[pl.ds(k * group + i * 32, 32)]
            for h in range(pixels // HALF):
                unpacked[pl.ds((h * group + i * 32) * 2 * bands, 512), :] = (
                    arrived[:, :, h * HALF : (h + 1) * HALF].reshape(512, HALF).astype(jnp.float32)
                )
        tag_rows = jnp.transpose(tags_in[pl.ds(k * group, group)].reshape(group, 128))
        code = lax.broadcasted_iota(jnp.int32, (codes, group), 0)
        chosen = jnp.concatenate(
            [(tag_rows[slot : slot + 1, :] == code).astype(jnp.bfloat16) for slot in range(2)],
            axis=1,
        )
        for b in range(bands):
            for h in range(pixels // HALF):
                values = jnp.concatenate(
                    [
                        unpacked[
                            pl.ds(
                                h * group * 2 * bands + slot * bands + b, group, stride=2 * bands
                            ),
                            :,
                        ]
                        for slot in range(2)
                    ],
                    axis=0,
                ).astype(jnp.bfloat16)
                lanes = pl.ds(b * pixels + h * HALF, HALF)
                added = jnp.dot(chosen, values, preferred_element_type=jnp.float32)
                if k == 0:
                    sums[:, lanes] = added
                else:
                    sums[:, lanes] += added

    picks = weights_ref.shape[0]
    for b in range(bands):
        lanes = pl.ds(b * pixels, pixels)
        total = None
        for pick in range(picks):
            rows = pl.ds(pick * 2 * cells, 2 * cells)
            term = jnp.dot(
                sums[rows, lanes].astype(jnp.bfloat16),
                weights_ref[pick],
                preferred_element_type=jnp.float32,
            )
            total = term if total is None else total + term
        resampled[:, lanes] = total

    @pl.loop(0, cells // 8)
    def _(g):
        start = pl.multiple_of(g * 8, 8)
        for b in range(bands):
            total = None
            for s in range(2):
                for other in range(bands):
                    term = (
                        mixing_ref[s, b * bands + other]
                        * resampled[
                            pl.ds(pl.multiple_of(s * cells + start, 8), 8),
                            pl.ds(other * pixels, pixels),
                        ]
                    )
                    total = term if total is None else total + term
            grid[pl.ds(pl.multiple_of(start + 8, 8), 8), pl.ds(b * pixels, pixels)] = total

    edge_out[0] = grid[pl.ds(8 + cells - 1, 1), :]
    edge_out[1] = grid[pl.ds(8, 1), :]
    copies = [
        pltpu.make_async_remote_copy(
            src_ref=edge_out.at[side],
            dst_ref=edge_in.at[side],
            send_sem=edge_send_sem.at[side],
            recv_sem=edge_recv_sem.at[side],
            device_id=(tile, (row + step) % 8),
            device_id_type=MESH,
        )
        for side, step in ((0, 1), (1, 7))
    ]
    for copy in copies:
        copy.start()
    for copy in copies:
        copy.wait()
    grid[pl.ds(7, 1), :] = jnp.where(row == 0, 0.0, edge_in[0])
    grid[pl.ds(8 + cells, 1), :] = jnp.where(row == 7, 0.0, edge_in[1])
    for g in range(cells // 16):
        above = grid[pl.ds(g * 16 + 7, 16), :]
        here = grid[pl.ds(g * 16 + 8, 16), :]
        below = grid[pl.ds(g * 16 + 9, 16), :]
        smoothed = 0.25 * above + 0.5 * here + 0.25 * below
        rows = pl.ds(g * 16, 16)
        out_ref[rows, :] = (smoothed * factor[rows, :]).astype(jnp.bfloat16)

    rest = pl.ds(1, devices - 1)
    pltpu.make_async_copy(outgoing.at[rest], outgoing.at[rest], send_sem).wait()
    pltpu.make_async_copy(tags_in.at[rest], tags_in.at[rest], tag_send_sem).wait()


def on_device(
    swath_blocks,
    footprint,
    cell_row,
    tile_pick,
    sensor,
    bandpass_offset,
    weight_tiles,
    lookup_table,
    lookup_bin,
    lookup_frac,
    brdf_params,
    vol_kernel,
    geo_kernel,
    clear_mask,
):
    devices = lax.axis_size("tile") * lax.axis_size("row")
    blocks = swath_blocks.shape[2]
    width = swath_blocks.shape[3]
    bands = bandpass_offset.shape[1]
    pixels = width // bands
    picks = weight_tiles.shape[0]
    cells = lookup_bin.shape[1]
    mixing = jnp.eye(bands, dtype=jnp.float32)[None, :, :] + bandpass_offset
    target = footprint.reshape(blocks)
    tag = (
        tile_pick.reshape(blocks) * 2 + sensor.reshape(blocks)
    ) * cells + cell_row.reshape(blocks)
    number = jnp.arange(blocks, dtype=jnp.int32)
    same = target[:, None] == target[None, :]
    earlier = number[:, None] > number[None, :]
    rank = jnp.sum(jnp.logical_and(same, earlier).astype(jnp.int32), axis=1)
    position = slot_of(target, rank, devices // CHUNKS)
    codes = picks * 2 * cells
    smem = pl.BlockSpec(memory_space=pltpu.SMEM)
    vmem = pl.BlockSpec(memory_space=pltpu.VMEM)
    f32 = jnp.float32
    result = pl.pallas_call(
        kernel,
        out_shape=jax.ShapeDtypeStruct((cells, width), jnp.bfloat16),
        in_specs=[smem] * 3 + [vmem] * 9,
        out_specs=vmem,
        scratch_shapes=[
            pltpu.VMEM((devices, 2 * bands, pixels), jnp.bfloat16),
            pltpu.VMEM((devices, 2 * bands, pixels), jnp.bfloat16),
            pltpu.VMEM((devices, 1, 128), jnp.int32),
            pltpu.VMEM((devices, 1, 128), jnp.int32),
            pltpu.VMEM((pixels // HALF * devices // CHUNKS * 2 * bands, HALF), f32),
            pltpu.VMEM((codes, width), f32),
            pltpu.VMEM((2 * cells, width), f32),
            pltpu.VMEM((cells + 16, width), f32),
            pltpu.VMEM((cells, width), f32),
            pltpu.VMEM((2, 1, width), f32),
            pltpu.VMEM((2, 1, width), f32),
            pltpu.SemaphoreType.DMA,
            pltpu.SemaphoreType.DMA((CHUNKS,)),
            pltpu.SemaphoreType.DMA,
            pltpu.SemaphoreType.DMA((CHUNKS,)),
            pltpu.SemaphoreType.DMA((2,)),
            pltpu.SemaphoreType.DMA((2,)),
        ],
        compiler_params=pltpu.CompilerParams(
            has_side_effects=True, vmem_limit_bytes=56 * 1024 * 1024
        ),
    )(
        mixing.reshape(2, bands * bands),
        lookup_table,
        brdf_params,
        swath_blocks.reshape(blocks, width),
        position.reshape(1, blocks),
        tag.reshape(1, blocks),
        weight_tiles,
        lookup_bin[0],
        lookup_frac[0],
        vol_kernel[0],
        geo_kernel[0],
        clear_mask[0],
    )
    return result[None]


def solution(mesh):
    in_specs = (
        P("tile", "row", None, None),
        P("tile", "row", None, None),
        P("tile", "row", None),
        P("tile", "row", None),
        P("tile", "row", None),
        P(),
        P(),
        P(),
        P("tile", "row", None),
        P("tile", "row", None),
        P(),
        P("tile", "row", None),
        P("tile", "row", None),
        P("tile", "row", None),
    )
    return jax.shard_map(
        on_device, mesh=mesh, in_specs=in_specs, out_specs=P("tile", "row", None), check_vma=False
    )
```

```python
import jax
import jax.numpy as jnp
from jax import lax
from jax.experimental import pallas as pl
from jax.experimental.pallas import tpu as pltpu
from jax.sharding import PartitionSpec as P

nadir_volume = 0.3
nadir_geometric = 0.6
MESH = pl.DeviceIdType.MESH
RING = 8
PEERS = 64
SLOTS = 16
HALF = 128
STREAMS = [(plan, pair, sign) for pair in range(2) for plan in range(2) for sign in (1, -1)]


def hops(pair, sign):
    return 4 if (pair == 0) == (sign > 0) else 3


def kernel(
    offset_ref,
    table_ref,
    brdf_ref,
    blocks_ref,
    target_ref,
    cell_ref,
    pick_ref,
    sensor_ref,
    weights_ref,
    bin_ref,
    frac_ref,
    vol_ref,
    geo_ref,
    mask_ref,
    out_ref,
    traits,
    spread,
    choose_out,
    choose_in,
    outgoing,
    incoming,
    tags_out,
    tags_in,
    sums,
    ring_out,
    ring_in,
    grid,
    factor,
    edge_out,
    edge_in,
    send_sem,
    recv_sem,
    tag_send_sem,
    tag_recv_sem,
    ring_send_sem,
    ring_recv_sem,
    edge_send_sem,
    edge_recv_sem,
):
    blocks = blocks_ref.shape[0]
    bands = 8
    pixels = 256
    cells = out_ref.shape[0]
    picks = weights_ref.shape[0] // pixels
    f32, bf16, i32 = jnp.float32, jnp.bfloat16, jnp.int32
    tile = lax.axis_index("tile")
    row = lax.axis_index("row")
    z, x, core = tile // 8, (tile // 2) % 4, tile % 2
    place = (row, z)

    def peer(plan, t):
        step = t % RING
        other = (t // RING + t) % RING
        side = ((x + other // 2) % 4) * 2 + (core + other % 2) % 2
        if plan == 0:
            return ((z + step) % 8) * 8 + side, row
        return z * 8 + side, (row + step) % 8

    target = target_ref[...]
    joined = ((target * 8 + pick_ref[...] * 2 + sensor_ref[...])).astype(f32)
    for j in range(blocks // 128):
        part = jnp.broadcast_to(joined[:, j * 128 : (j + 1) * 128], (128, 128))
        traits[pl.ds(j * 128, 128), :] = jnp.transpose(part).astype(i32)
    rank_parts = []
    own_target = traits[...] >> 3
    first = lax.broadcasted_iota(i32, (blocks, 128), 0)
    for j in range(blocks // 128):
        second = lax.broadcasted_iota(i32, (blocks, 128), 1) + j * 128
        same = (own_target == target[:, j * 128 : (j + 1) * 128]) & (first < second)
        rank_parts.append(jnp.sum(same.astype(f32), axis=0, keepdims=True))
    rank = jnp.concatenate(rank_parts, axis=1).astype(i32)

    to_row = target & 7
    to_z = target >> 6
    to_x = (target >> 4) & 3
    to_core = (target >> 3) & 1
    other = ((to_x - x) & 3) * 2 + ((to_core - core) & 1)
    for plan in range(2):
        step = ((to_z - z) & 7) if plan == 0 else ((to_row - row) & 7)
        number = ((other - step) & 7) * 8 + step
        slot = (to_row if plan == 0 else to_z) * 2 + rank
        position = number * SLOTS + slot
        for i in range(PEERS * SLOTS // 128):
            here = lax.broadcasted_iota(i32, (128, blocks), 0) + i * 128
            choose_out[plan, pl.ds(i * 128, 128), :] = (position == here).astype(f32).astype(bf16)
        to_peer = (lax.broadcasted_iota(i32, (PEERS, blocks), 0) == number).astype(f32).astype(bf16)
        lane_slot = lax.broadcasted_iota(i32, (128, blocks), 0) & (SLOTS - 1)
        marks = jnp.where(lane_slot == slot, cell_ref[...] + 1, 0).astype(f32).astype(bf16)
        found = lax.dot_general(
            to_peer, marks, (((1,), (1,)), ((), ())), preferred_element_type=f32
        )
        lane = lax.broadcasted_iota(i32, (PEERS, 128), 1) & (SLOTS - 1)
        base = ((lane >> 1) * cells - 1).astype(f32)
        tags_out[plan] = jnp.where(found > 0.0, base + found, -1.0).reshape(PEERS, 1, 128)
        tags_in[plan, 0] = tags_out[plan, 0]

    @pl.loop(1, PEERS)
    def _(t):
        for plan in range(2):
            pltpu.make_async_remote_copy(
                src_ref=tags_out.at[plan, t],
                dst_ref=tags_in.at[plan, t],
                send_sem=tag_send_sem.at[plan],
                recv_sem=tag_recv_sem.at[plan],
                device_id=peer(plan, t),
                device_id_type=MESH,
            ).start()

    for first_band in range(4):
        pair_bands = (first_band, first_band + 4)

        @pl.loop(0, blocks // 64)
        def _(g):
            rows = pl.ds(pl.multiple_of(g * 64, 64), 64)
            trait = traits[rows, :]
            is_second = (trait & 1) == 1
            pick = (trait >> 1) & 3
            for h in range(pixels // HALF):
                totals = [None, None]
                for other in range(bands):
                    value = blocks_ref[rows, pl.ds(other * pixels + h * HALF, HALF)].astype(f32)
                    for plan in range(2):
                        band = pair_bands[plan]
                        own = 1.0 if band == other else 0.0
                        mix = jnp.where(
                            is_second,
                            own + offset_ref[1, band, other],
                            own + offset_ref[0, band, other],
                        )
                        term = mix * value
                        totals[plan] = term if other == 0 else totals[plan] + term
                for plan in range(2):
                    for k in range(picks):
                        spread[plan, rows, pl.ds(k * pixels + h * HALF, HALF)] = jnp.where(
                            pick == k, totals[plan], 0.0
                        ).astype(bf16)

        for plan in range(2):
            band = pair_bands[plan]
            resampled = jnp.dot(
                spread[plan], weights_ref[...], preferred_element_type=f32
            ).astype(bf16)
            moved = jnp.dot(choose_out[plan], resampled, preferred_element_type=f32)
            outgoing[band] = moved.astype(bf16).reshape(PEERS, SLOTS, pixels)
            incoming[band, 0] = outgoing[band, 0]

        @pl.loop(1, PEERS)
        def _(t):
            for plan in range(2):
                band = pair_bands[plan]
                pltpu.make_async_remote_copy(
                    src_ref=outgoing.at[band, t],
                    dst_ref=incoming.at[band, t],
                    send_sem=send_sem.at[band],
                    recv_sem=recv_sem.at[band],
                    device_id=peer(plan, t),
                    device_id_type=MESH,
                ).start()

    bins = table_ref.shape[1] - 1

    @pl.loop(0, cells // 8)
    def _(g):
        rows = pl.ds(pl.multiple_of(g * 8, 8), 8)
        which = bin_ref[rows, :]
        part = frac_ref[rows, :]
        volume_angle = vol_ref[rows, :]
        geometric_angle = geo_ref[rows, :]
        keep = mask_ref[rows, :].astype(f32)
        lower = [jnp.full((8, pixels), table_ref[b, 0]) for b in range(bands)]
        upper = [jnp.full((8, pixels), table_ref[b, 1]) for b in range(bands)]
        for n in range(1, bins):
            here = which == n
            for b in range(bands):
                lower[b] = jnp.where(here, table_ref[b, n], lower[b])
                upper[b] = jnp.where(here, table_ref[b, n + 1], upper[b])
        for b in range(bands):
            value = lower[b] * (1.0 - part) + upper[b] * part
            isotropic, volume, geometric = brdf_ref[0, b], brdf_ref[1, b], brdf_ref[2, b]
            numerator = isotropic + volume * nadir_volume + geometric * nadir_geometric
            denominator = isotropic + volume * volume_angle + geometric * geometric_angle
            factor[rows, pl.ds(b * pixels, pixels)] = value * (numerator / denominator) * keep

    rest = pl.ds(1, PEERS - 1)
    sublane = lax.broadcasted_iota(i32, (8, 128), 0)
    lane_group = lax.broadcasted_iota(i32, (8, 128), 1) >> 4
    line = lax.broadcasted_iota(i32, (RING * cells, 128), 0).astype(f32)
    for plan in range(2):
        pltpu.make_async_copy(
            tags_in.at[plan, rest], tags_in.at[plan, rest], tag_recv_sem.at[plan]
        ).wait()
        arrived = tags_in[plan].reshape(PEERS, 128)
        for g in range(PEERS // 8):
            code = jnp.sum(
                jnp.where(sublane == lane_group, arrived[g * 8 : (g + 1) * 8], 0.0),
                axis=0,
                keepdims=True,
            )
            choose_in[plan, :, pl.ds(g * 128, 128)] = (line == code).astype(f32).astype(bf16)

    def gather_pair(plan, pair):
        for band in (plan * 4 + pair * 2, plan * 4 + pair * 2 + 1):
            pltpu.make_async_copy(
                incoming.at[band, rest], incoming.at[band, rest], recv_sem.at[band]
            ).wait()
            sums[band] = jnp.dot(
                choose_in[plan],
                incoming[band].reshape(PEERS * SLOTS, pixels),
                preferred_element_type=f32,
            )

    def ring_copy(plan, pair, sign, step):
        stream = STREAMS.index((plan, pair, sign))
        if plan == 0:
            device = (tile, (row + sign + 8) % 8)
        else:
            device = (((z + sign + 8) % 8) * 8 + x * 2 + core, row)
        return pltpu.make_async_remote_copy(
            src_ref=ring_out.at[stream, step],
            dst_ref=ring_in.at[stream, step],
            send_sem=ring_send_sem.at[stream, step],
            recv_sem=ring_recv_sem.at[stream, step],
            device_id=device,
            device_id_type=MESH,
        )

    def ring_step(pair, step):
        for plan in range(2):
            if step == 0:
                gather_pair(plan, pair)
            for sign in (1, -1):
                length = hops(pair, sign)
                if step >= length:
                    continue
                stream = STREAMS.index((plan, pair, sign))
                toward = (place[plan] + sign * (length - step) + 8) % 8
                lines = pl.ds(pl.multiple_of(toward * cells, cells), cells)
                if step > 0:
                    ring_copy(plan, pair, sign, step - 1).wait_recv()
                for i in range(2):
                    value = sums[plan * 4 + pair * 2 + i, lines, :]
                    if step > 0:
                        value = value + ring_in[stream, step - 1, i].astype(f32)
                    ring_out[stream, step, i] = value.astype(bf16)
                ring_copy(plan, pair, sign, step).start()

    def finish(pair):
        for plan in range(2):
            lines = pl.ds(pl.multiple_of(place[plan] * cells, cells), cells)
            for sign in (1, -1):
                ring_copy(plan, pair, sign, hops(pair, sign) - 1).wait_recv()
            for i in range(2):
                band = plan * 4 + pair * 2 + i
                total = sums[band, lines, :]
                for sign in (1, -1):
                    stream = STREAMS.index((plan, pair, sign))
                    total = total + ring_in[stream, hops(pair, sign) - 1, i].astype(f32)
                grid[pl.ds(8, cells), pl.ds(band * pixels, pixels)] = total

    ring_step(0, 0)
    ring_step(0, 1)
    ring_step(1, 0)
    ring_step(0, 2)
    ring_step(1, 1)
    ring_step(0, 3)
    ring_step(1, 2)
    finish(0)
    ring_step(1, 3)
    finish(1)

    edge_out[0] = grid[pl.ds(8 + cells - 1, 1), :]
    edge_out[1] = grid[pl.ds(8, 1), :]
    copies = [
        pltpu.make_async_remote_copy(
            src_ref=edge_out.at[side],
            dst_ref=edge_in.at[side],
            send_sem=edge_send_sem.at[side],
            recv_sem=edge_recv_sem.at[side],
            device_id=(tile, (row + step) % 8),
            device_id_type=MESH,
        )
        for side, step in ((0, 1), (1, 7))
    ]
    for copy in copies:
        copy.start()
    for plan in range(2):
        pltpu.make_async_copy(
            tags_out.at[plan, rest], tags_out.at[plan, rest], tag_send_sem.at[plan]
        ).wait()
    for band in range(bands):
        pltpu.make_async_copy(
            outgoing.at[band, rest], outgoing.at[band, rest], send_sem.at[band]
        ).wait()
    for plan, pair, sign in STREAMS:
        for step in range(hops(pair, sign)):
            ring_copy(plan, pair, sign, step).wait_send()
    for copy in copies:
        copy.wait()
    grid[pl.ds(7, 1), :] = jnp.where(row == 0, 0.0, edge_in[0])
    grid[pl.ds(8 + cells, 1), :] = jnp.where(row == 7, 0.0, edge_in[1])
    for g in range(cells // 16):
        above = grid[pl.ds(g * 16 + 7, 16), :]
        here = grid[pl.ds(g * 16 + 8, 16), :]
        below = grid[pl.ds(g * 16 + 9, 16), :]
        smoothed = 0.25 * above + 0.5 * here + 0.25 * below
        rows = pl.ds(g * 16, 16)
        out_ref[rows, :] = (smoothed * factor[rows, :]).astype(bf16)


def on_device(
    swath_blocks,
    footprint,
    cell_row,
    tile_pick,
    sensor,
    bandpass_offset,
    weight_tiles,
    lookup_table,
    lookup_bin,
    lookup_frac,
    brdf_params,
    vol_kernel,
    geo_kernel,
    clear_mask,
):
    blocks = swath_blocks.shape[2]
    width = swath_blocks.shape[3]
    bands = bandpass_offset.shape[1]
    pixels = width // bands
    picks = weight_tiles.shape[0]
    cells = lookup_bin.shape[1]
    smem = pl.BlockSpec(memory_space=pltpu.SMEM)
    vmem = pl.BlockSpec(memory_space=pltpu.VMEM)
    f32, bf16 = jnp.float32, jnp.bfloat16
    dma = pltpu.SemaphoreType.DMA
    result = pl.pallas_call(
        kernel,
        out_shape=jax.ShapeDtypeStruct((cells, width), bf16),
        in_specs=[smem] * 3 + [vmem] * 11,
        out_specs=vmem,
        scratch_shapes=[
            pltpu.VMEM((blocks, 128), jnp.int32),
            pltpu.VMEM((2, blocks, picks * pixels), bf16),
            pltpu.VMEM((2, PEERS * SLOTS, blocks), bf16),
            pltpu.VMEM((2, RING * cells, PEERS * SLOTS), bf16),
            pltpu.VMEM((bands, PEERS, SLOTS, pixels), bf16),
            pltpu.VMEM((bands, PEERS, SLOTS, pixels), bf16),
            pltpu.VMEM((2, PEERS, 1, 128), f32),
            pltpu.VMEM((2, PEERS, 1, 128), f32),
            pltpu.VMEM((bands, RING * cells, pixels), f32),
            pltpu.VMEM((len(STREAMS), 4, 2, cells, pixels), bf16),
            pltpu.VMEM((len(STREAMS), 4, 2, cells, pixels), bf16),
            pltpu.VMEM((cells + 16, width), f32),
            pltpu.VMEM((cells, width), f32),
            pltpu.VMEM((2, 1, width), f32),
            pltpu.VMEM((2, 1, width), f32),
            dma((bands,)),
            dma((bands,)),
            dma((2,)),
            dma((2,)),
            dma((len(STREAMS), 4)),
            dma((len(STREAMS), 4)),
            dma((2,)),
            dma((2,)),
        ],
        compiler_params=pltpu.CompilerParams(
            has_side_effects=True, vmem_limit_bytes=58 * 1024 * 1024
        ),
    )(
        bandpass_offset,
        lookup_table,
        brdf_params.T,
        swath_blocks.reshape(blocks, width),
        footprint.reshape(1, blocks),
        cell_row.reshape(1, blocks),
        tile_pick.reshape(1, blocks),
        sensor.reshape(1, blocks),
        weight_tiles.reshape(picks * pixels, pixels),
        lookup_bin[0],
        lookup_frac[0],
        vol_kernel[0],
        geo_kernel[0],
        clear_mask[0],
    )
    return result[None]


def solution(mesh):
    in_specs = (
        P("tile", "row", None, None),
        P("tile", "row", None, None),
        P("tile", "row", None),
        P("tile", "row", None),
        P("tile", "row", None),
        P(),
        P(),
        P(),
        P("tile", "row", None),
        P("tile", "row", None),
        P(),
        P("tile", "row", None),
        P("tile", "row", None),
        P("tile", "row", None),
    )
    return jax.shard_map(
        on_device, mesh=mesh, in_specs=in_specs, out_specs=P("tile", "row", None), check_vma=False
    )
```

```python
import jax
import jax.numpy as jnp
from jax import lax
from jax.experimental import pallas as pl
from jax.experimental.pallas import tpu as pltpu
from jax.sharding import PartitionSpec as P

nadir_volume = 0.3
nadir_geometric = 0.6
MESH = pl.DeviceIdType.MESH
RING = 8
PEERS = 64
SLOTS = 16
HALF = 128
STREAMS = [(plan, pair, sign) for pair in range(2) for plan in range(2) for sign in (1, -1)]


def hops(pair, sign):
    return 4 if (pair == 0) == (sign > 0) else 3


def kernel(
    offset_ref,
    table_ref,
    brdf_ref,
    blocks_ref,
    target_ref,
    cell_ref,
    pick_ref,
    sensor_ref,
    weights_ref,
    bin_ref,
    frac_ref,
    vol_ref,
    geo_ref,
    mask_ref,
    out_ref,
    traits,
    spread,
    choose_out,
    choose_in,
    outgoing,
    incoming,
    tags_out,
    tags_in,
    sums,
    ring_out,
    ring_in,
    grid,
    factor,
    edge_out,
    edge_in,
    send_sem,
    recv_sem,
    tag_send_sem,
    tag_recv_sem,
    ring_send_sem,
    ring_recv_sem,
    edge_send_sem,
    edge_recv_sem,
    beside_sem,
):
    blocks = blocks_ref.shape[0]
    bands = 8
    pixels = 256
    cells = out_ref.shape[0]
    picks = weights_ref.shape[0] // pixels
    f32, bf16, i32 = jnp.float32, jnp.bfloat16, jnp.int32
    tile = lax.axis_index("tile")
    row = lax.axis_index("row")
    z, x, core = tile // 8, (tile // 2) % 4, tile % 2
    place = (row, z)

    def peer(plan, t):
        step = t % RING
        other = (t // RING + t) % RING
        side = ((x + other // 2) % 4) * 2 + (core + other % 2) % 2
        if plan == 0:
            return ((z + step) % 8) * 8 + side, row
        return z * 8 + side, (row + step) % 8

    around = pltpu.get_barrier_semaphore()
    for step in range(1, 8):
        side = ((x + step // 2) % 4) * 2 + (core + step % 2) % 2
        for device in (
            (((z + step) % 8) * 8 + x * 2 + core, row),
            (tile, (row + step) % 8),
            (z * 8 + side, row),
        ):
            pl.semaphore_signal(around, inc=1, device_id=device, device_id_type=MESH)

    target = target_ref[...]
    joined = ((target * 8 + pick_ref[...] * 2 + sensor_ref[...])).astype(f32)
    for j in range(blocks // 128):
        part = jnp.broadcast_to(joined[:, j * 128 : (j + 1) * 128], (128, 128))
        traits[pl.ds(j * 128, 128), :] = jnp.transpose(part).astype(i32)
    rank_parts = []
    own_target = traits[...] >> 3
    first = lax.broadcasted_iota(i32, (blocks, 128), 0)
    for j in range(blocks // 128):
        second = lax.broadcasted_iota(i32, (blocks, 128), 1) + j * 128
        same = (own_target == target[:, j * 128 : (j + 1) * 128]) & (first < second)
        rank_parts.append(jnp.sum(same.astype(f32), axis=0, keepdims=True))
    rank = jnp.concatenate(rank_parts, axis=1).astype(i32)

    to_row = target & 7
    to_z = target >> 6
    to_x = (target >> 4) & 3
    to_core = (target >> 3) & 1
    other = ((to_x - x) & 3) * 2 + ((to_core - core) & 1)
    for plan in range(2):
        step = ((to_z - z) & 7) if plan == 0 else ((to_row - row) & 7)
        number = ((other - step) & 7) * 8 + step
        slot = (to_row if plan == 0 else to_z) * 2 + rank
        position = number * SLOTS + slot
        for i in range(PEERS * SLOTS // 128):
            here = lax.broadcasted_iota(i32, (128, blocks), 0) + i * 128
            choose_out[plan, pl.ds(i * 128, 128), :] = (position == here).astype(f32).astype(bf16)
        to_peer = (lax.broadcasted_iota(i32, (PEERS, blocks), 0) == number).astype(f32).astype(bf16)
        lane_slot = lax.broadcasted_iota(i32, (128, blocks), 0) & (SLOTS - 1)
        marks = jnp.where(lane_slot == slot, cell_ref[...] + 1, 0).astype(f32).astype(bf16)
        found = lax.dot_general(
            to_peer, marks, (((1,), (1,)), ((), ())), preferred_element_type=f32
        )
        lane = lax.broadcasted_iota(i32, (PEERS, 128), 1) & (SLOTS - 1)
        base = ((lane >> 1) * cells - 1).astype(f32)
        tags_out[plan] = jnp.where(found > 0.0, base + found, -1.0).reshape(PEERS, 1, 128)
        tags_in[plan, 0] = tags_out[plan, 0]

    pl.semaphore_wait(around, 21)
    for step in range(1, 8):
        side = ((x + step // 2) % 4) * 2 + (core + step % 2) % 2
        pl.semaphore_signal(
            beside_sem, inc=1, device_id=(z * 8 + side, row), device_id_type=MESH
        )

    for first_band in range(4):
        pair_bands = (first_band, first_band + 4)

        @pl.loop(0, blocks // 64)
        def _(g):
            rows = pl.ds(pl.multiple_of(g * 64, 64), 64)
            trait = traits[rows, :]
            is_second = (trait & 1) == 1
            pick = (trait >> 1) & 3
            for h in range(pixels // HALF):
                totals = [None, None]
                for other in range(bands):
                    value = blocks_ref[rows, pl.ds(other * pixels + h * HALF, HALF)].astype(f32)
                    for plan in range(2):
                        band = pair_bands[plan]
                        own = 1.0 if band == other else 0.0
                        mix = jnp.where(
                            is_second,
                            own + offset_ref[1, band, other],
                            own + offset_ref[0, band, other],
                        )
                        term = mix * value
                        totals[plan] = term if other == 0 else totals[plan] + term
                for plan in range(2):
                    for k in range(picks):
                        spread[plan, rows, pl.ds(k * pixels + h * HALF, HALF)] = jnp.where(
                            pick == k, totals[plan], 0.0
                        ).astype(bf16)

        for plan in range(2):
            band = pair_bands[plan]
            resampled = jnp.dot(
                spread[plan], weights_ref[...], preferred_element_type=f32
            ).astype(bf16)
            moved = jnp.dot(choose_out[plan], resampled, preferred_element_type=f32)
            outgoing[band] = moved.astype(bf16).reshape(PEERS, SLOTS, pixels)
            incoming[band, 0] = outgoing[band, 0]

        if first_band == 0:
            pl.semaphore_wait(beside_sem, 7)

        @pl.loop(1, PEERS)
        def _(t):
            for plan in range(2):
                band = pair_bands[plan]
                pltpu.make_async_remote_copy(
                    src_ref=outgoing.at[band, t],
                    dst_ref=incoming.at[band, t],
                    send_sem=send_sem.at[band],
                    recv_sem=recv_sem.at[band],
                    device_id=peer(plan, t),
                    device_id_type=MESH,
                ).start()

        if first_band == 0:

            @pl.loop(1, PEERS)
            def _(t):
                for plan in range(2):
                    pltpu.make_async_remote_copy(
                        src_ref=tags_out.at[plan, t],
                        dst_ref=tags_in.at[plan, t],
                        send_sem=tag_send_sem.at[plan],
                        recv_sem=tag_recv_sem.at[plan],
                        device_id=peer(plan, t),
                        device_id_type=MESH,
                    ).start()

    bins = table_ref.shape[1] - 1

    @pl.loop(0, cells // 8)
    def _(g):
        rows = pl.ds(pl.multiple_of(g * 8, 8), 8)
        which = bin_ref[rows, :]
        part = frac_ref[rows, :]
        volume_angle = vol_ref[rows, :]
        geometric_angle = geo_ref[rows, :]
        keep = mask_ref[rows, :].astype(f32)
        lower = [jnp.full((8, pixels), table_ref[b, 0]) for b in range(bands)]
        upper = [jnp.full((8, pixels), table_ref[b, 1]) for b in range(bands)]
        for n in range(1, bins):
            here = which == n
            for b in range(bands):
                lower[b] = jnp.where(here, table_ref[b, n], lower[b])
                upper[b] = jnp.where(here, table_ref[b, n + 1], upper[b])
        for b in range(bands):
            value = lower[b] * (1.0 - part) + upper[b] * part
            isotropic, volume, geometric = brdf_ref[0, b], brdf_ref[1, b], brdf_ref[2, b]
            numerator = isotropic + volume * nadir_volume + geometric * nadir_geometric
            denominator = isotropic + volume * volume_angle + geometric * geometric_angle
            factor[rows, pl.ds(b * pixels, pixels)] = value * (numerator / denominator) * keep

    rest = pl.ds(1, PEERS - 1)
    sublane = lax.broadcasted_iota(i32, (8, 128), 0)
    lane_group = lax.broadcasted_iota(i32, (8, 128), 1) >> 4
    line = lax.broadcasted_iota(i32, (RING * cells, 128), 0).astype(f32)
    for plan in range(2):
        pltpu.make_async_copy(
            tags_in.at[plan, rest], tags_in.at[plan, rest], tag_recv_sem.at[plan]
        ).wait()
        arrived = tags_in[plan].reshape(PEERS, 128)
        for g in range(PEERS // 8):
            code = jnp.sum(
                jnp.where(sublane == lane_group, arrived[g * 8 : (g + 1) * 8], 0.0),
                axis=0,
                keepdims=True,
            )
            choose_in[plan, :, pl.ds(g * 128, 128)] = (line == code).astype(f32).astype(bf16)

    def gather_pair(plan, pair):
        for band in (plan * 4 + pair * 2, plan * 4 + pair * 2 + 1):
            pltpu.make_async_copy(
                incoming.at[band, rest], incoming.at[band, rest], recv_sem.at[band]
            ).wait()
            sums[band] = jnp.dot(
                choose_in[plan],
                incoming[band].reshape(PEERS * SLOTS, pixels),
                preferred_element_type=f32,
            )

    def ring_copy(plan, pair, sign, step):
        stream = STREAMS.index((plan, pair, sign))
        if plan == 0:
            device = (tile, (row + sign + 8) % 8)
        else:
            device = (((z + sign + 8) % 8) * 8 + x * 2 + core, row)
        return pltpu.make_async_remote_copy(
            src_ref=ring_out.at[stream, step],
            dst_ref=ring_in.at[stream, step],
            send_sem=ring_send_sem.at[stream, step],
            recv_sem=ring_recv_sem.at[stream, step],
            device_id=device,
            device_id_type=MESH,
        )

    def ring_step(pair, step):
        for plan in range(2):
            if step == 0:
                gather_pair(plan, pair)
            for sign in (1, -1):
                length = hops(pair, sign)
                if step >= length:
                    continue
                stream = STREAMS.index((plan, pair, sign))
                toward = (place[plan] + sign * (length - step) + 8) % 8
                lines = pl.ds(pl.multiple_of(toward * cells, cells), cells)
                if step > 0:
                    ring_copy(plan, pair, sign, step - 1).wait_recv()
                for i in range(2):
                    value = sums[plan * 4 + pair * 2 + i, lines, :]
                    if step > 0:
                        value = value + ring_in[stream, step - 1, i].astype(f32)
                    ring_out[stream, step, i] = value.astype(bf16)
                ring_copy(plan, pair, sign, step).start()

    def finish(pair):
        for plan in range(2):
            lines = pl.ds(pl.multiple_of(place[plan] * cells, cells), cells)
            for sign in (1, -1):
                ring_copy(plan, pair, sign, hops(pair, sign) - 1).wait_recv()
            for i in range(2):
                band = plan * 4 + pair * 2 + i
                total = sums[band, lines, :]
                for sign in (1, -1):
                    stream = STREAMS.index((plan, pair, sign))
                    total = total + ring_in[stream, hops(pair, sign) - 1, i].astype(f32)
                grid[pl.ds(8, cells), pl.ds(band * pixels, pixels)] = total

    ring_step(0, 0)
    ring_step(0, 1)
    ring_step(1, 0)
    ring_step(0, 2)
    ring_step(1, 1)
    ring_step(0, 3)
    ring_step(1, 2)
    finish(0)
    ring_step(1, 3)
    finish(1)

    edge_out[0] = grid[pl.ds(8 + cells - 1, 1), :]
    edge_out[1] = grid[pl.ds(8, 1), :]
    copies = [
        pltpu.make_async_remote_copy(
            src_ref=edge_out.at[side],
            dst_ref=edge_in.at[side],
            send_sem=edge_send_sem.at[side],
            recv_sem=edge_recv_sem.at[side],
            device_id=(tile, (row + step) % 8),
            device_id_type=MESH,
        )
        for side, step in ((0, 1), (1, 7))
    ]
    for copy in copies:
        copy.start()
    for plan in range(2):
        pltpu.make_async_copy(
            tags_out.at[plan, rest], tags_out.at[plan, rest], tag_send_sem.at[plan]
        ).wait()
    for band in range(bands):
        pltpu.make_async_copy(
            outgoing.at[band, rest], outgoing.at[band, rest], send_sem.at[band]
        ).wait()
    for plan, pair, sign in STREAMS:
        for step in range(hops(pair, sign)):
            ring_copy(plan, pair, sign, step).wait_send()
    for copy in copies:
        copy.wait()
    grid[pl.ds(7, 1), :] = jnp.where(row == 0, 0.0, edge_in[0])
    grid[pl.ds(8 + cells, 1), :] = jnp.where(row == 7, 0.0, edge_in[1])
    for g in range(cells // 16):
        above = grid[pl.ds(g * 16 + 7, 16), :]
        here = grid[pl.ds(g * 16 + 8, 16), :]
        below = grid[pl.ds(g * 16 + 9, 16), :]
        smoothed = 0.25 * above + 0.5 * here + 0.25 * below
        rows = pl.ds(g * 16, 16)
        out_ref[rows, :] = (smoothed * factor[rows, :]).astype(bf16)


def on_device(
    swath_blocks,
    footprint,
    cell_row,
    tile_pick,
    sensor,
    bandpass_offset,
    weight_tiles,
    lookup_table,
    lookup_bin,
    lookup_frac,
    brdf_params,
    vol_kernel,
    geo_kernel,
    clear_mask,
):
    blocks = swath_blocks.shape[2]
    width = swath_blocks.shape[3]
    bands = bandpass_offset.shape[1]
    pixels = width // bands
    picks = weight_tiles.shape[0]
    cells = lookup_bin.shape[1]
    smem = pl.BlockSpec(memory_space=pltpu.SMEM)
    vmem = pl.BlockSpec(memory_space=pltpu.VMEM)
    f32, bf16 = jnp.float32, jnp.bfloat16
    dma = pltpu.SemaphoreType.DMA
    result = pl.pallas_call(
        kernel,
        out_shape=jax.ShapeDtypeStruct((cells, width), bf16),
        in_specs=[smem] * 3 + [vmem] * 11,
        out_specs=vmem,
        scratch_shapes=[
            pltpu.VMEM((blocks, 128), jnp.int32),
            pltpu.VMEM((2, blocks, picks * pixels), bf16),
            pltpu.VMEM((2, PEERS * SLOTS, blocks), bf16),
            pltpu.VMEM((2, RING * cells, PEERS * SLOTS), bf16),
            pltpu.VMEM((bands, PEERS, SLOTS, pixels), bf16),
            pltpu.VMEM((bands, PEERS, SLOTS, pixels), bf16),
            pltpu.VMEM((2, PEERS, 1, 128), f32),
            pltpu.VMEM((2, PEERS, 1, 128), f32),
            pltpu.VMEM((bands, RING * cells, pixels), f32),
            pltpu.VMEM((len(STREAMS), 4, 2, cells, pixels), bf16),
            pltpu.VMEM((len(STREAMS), 4, 2, cells, pixels), bf16),
            pltpu.VMEM((cells + 16, width), f32),
            pltpu.VMEM((cells, width), f32),
            pltpu.VMEM((2, 1, width), f32),
            pltpu.VMEM((2, 1, width), f32),
            dma((bands,)),
            dma((bands,)),
            dma((2,)),
            dma((2,)),
            dma((len(STREAMS), 4)),
            dma((len(STREAMS), 4)),
            dma((2,)),
            dma((2,)),
            pltpu.SemaphoreType.REGULAR,
        ],
        compiler_params=pltpu.CompilerParams(
            has_side_effects=True, collective_id=0, vmem_limit_bytes=58 * 1024 * 1024
        ),
    )(
        bandpass_offset,
        lookup_table,
        brdf_params.T,
        swath_blocks.reshape(blocks, width),
        footprint.reshape(1, blocks),
        cell_row.reshape(1, blocks),
        tile_pick.reshape(1, blocks),
        sensor.reshape(1, blocks),
        weight_tiles.reshape(picks * pixels, pixels),
        lookup_bin[0],
        lookup_frac[0],
        vol_kernel[0],
        geo_kernel[0],
        clear_mask[0],
    )
    return result[None]


def solution(mesh):
    in_specs = (
        P("tile", "row", None, None),
        P("tile", "row", None, None),
        P("tile", "row", None),
        P("tile", "row", None),
        P("tile", "row", None),
        P(),
        P(),
        P(),
        P("tile", "row", None),
        P("tile", "row", None),
        P(),
        P("tile", "row", None),
        P("tile", "row", None),
        P("tile", "row", None),
    )
    return jax.shard_map(
        on_device, mesh=mesh, in_specs=in_specs, out_specs=P("tile", "row", None), check_vma=False
    )
```

```python
import jax
import jax.numpy as jnp
from jax import lax
from jax.experimental import pallas as pl
from jax.experimental.pallas import tpu as pltpu
from jax.sharding import PartitionSpec as P

nadir_volume = 0.3
nadir_geometric = 0.6
MESH = pl.DeviceIdType.MESH
RING = 8
PEERS = 64
SLOTS = 16
HALF = 128
STREAMS = [(plan, pair, sign) for pair in range(2) for plan in range(2) for sign in (1, -1)]


def hops(pair, sign):
    return 4 if (pair == 0) == (sign > 0) else 3


def kernel(
    offset_ref,
    table_ref,
    brdf_ref,
    blocks_hbm,
    target_ref,
    cell_ref,
    pick_ref,
    sensor_ref,
    weights_hbm,
    bin_hbm,
    frac_hbm,
    vol_hbm,
    geo_hbm,
    mask_hbm,
    out_ref,
    blocks_ref,
    weights_ref,
    bin_ref,
    frac_ref,
    vol_ref,
    geo_ref,
    mask_ref,
    traits,
    spread,
    choose_out,
    choose_in,
    outgoing,
    incoming,
    tags_out,
    tags_in,
    sums,
    ring_out,
    ring_in,
    grid,
    factor,
    edge_out,
    edge_in,
    send_sem,
    recv_sem,
    tag_send_sem,
    tag_recv_sem,
    ring_send_sem,
    ring_recv_sem,
    edge_send_sem,
    edge_recv_sem,
    beside_sem,
    load_sem,
):
    blocks = blocks_ref.shape[0]
    bands = 8
    pixels = 256
    cells = out_ref.shape[0]
    picks = weights_ref.shape[0] // pixels
    f32, bf16, i32 = jnp.float32, jnp.bfloat16, jnp.int32
    tile = lax.axis_index("tile")
    row = lax.axis_index("row")
    z, x, core = tile // 8, (tile // 2) % 4, tile % 2
    place = (row, z)

    def peer(plan, t):
        step = t % RING
        other = (t // RING + t) % RING
        side = ((x + other // 2) % 4) * 2 + (core + other % 2) % 2
        if plan == 0:
            return ((z + step) % 8) * 8 + side, row
        return z * 8 + side, (row + step) % 8

    around = pltpu.get_barrier_semaphore()
    for step in range(1, 8):
        side = ((x + step // 2) % 4) * 2 + (core + step % 2) % 2
        for device in (
            (((z + step) % 8) * 8 + x * 2 + core, row),
            (tile, (row + step) % 8),
            (z * 8 + side, row),
        ):
            pl.semaphore_signal(around, inc=1, device_id=device, device_id_type=MESH)
    loads = [
        pltpu.make_async_copy(source, kept, load_sem.at[i])
        for i, (source, kept) in enumerate(
            (
                (blocks_hbm, blocks_ref),
                (weights_hbm, weights_ref),
                (bin_hbm, bin_ref),
                (frac_hbm, frac_ref),
                (vol_hbm, vol_ref),
                (geo_hbm, geo_ref),
                (mask_hbm, mask_ref),
            )
        )
    ]
    for load in loads:
        load.start()

    target = target_ref[...]
    joined = ((target * 8 + pick_ref[...] * 2 + sensor_ref[...])).astype(f32)
    for j in range(blocks // 128):
        part = jnp.broadcast_to(joined[:, j * 128 : (j + 1) * 128], (128, 128))
        traits[pl.ds(j * 128, 128), :] = jnp.transpose(part).astype(i32)
    rank_parts = []
    own_target = traits[...] >> 3
    first = lax.broadcasted_iota(i32, (blocks, 128), 0)
    for j in range(blocks // 128):
        second = lax.broadcasted_iota(i32, (blocks, 128), 1) + j * 128
        same = (own_target == target[:, j * 128 : (j + 1) * 128]) & (first < second)
        rank_parts.append(jnp.sum(same.astype(f32), axis=0, keepdims=True))
    rank = jnp.concatenate(rank_parts, axis=1).astype(i32)

    to_row = target & 7
    to_z = target >> 6
    to_x = (target >> 4) & 3
    to_core = (target >> 3) & 1
    other = ((to_x - x) & 3) * 2 + ((to_core - core) & 1)
    numbers, slots = [], []
    for plan in range(2):
        step = ((to_z - z) & 7) if plan == 0 else ((to_row - row) & 7)
        number = ((other - step) & 7) * 8 + step
        slot = (to_row if plan == 0 else to_z) * 2 + rank
        position = number * SLOTS + slot
        for i in range(PEERS * SLOTS // 128):
            here = lax.broadcasted_iota(i32, (128, blocks), 0) + i * 128
            choose_out[plan, pl.ds(i * 128, 128), :] = (position == here).astype(f32).astype(bf16)
        numbers.append(number)
        slots.append(slot)

    pl.semaphore_wait(around, 21)
    for step in range(1, 8):
        side = ((x + step // 2) % 4) * 2 + (core + step % 2) % 2
        pl.semaphore_signal(
            beside_sem, inc=1, device_id=(z * 8 + side, row), device_id_type=MESH
        )

    loads[0].wait()
    loads[1].wait()
    for first_band in range(4):
        pair_bands = (first_band, first_band + 4)

        @pl.loop(0, blocks // 64)
        def _(g):
            rows = pl.ds(pl.multiple_of(g * 64, 64), 64)
            trait = traits[rows, :]
            is_second = (trait & 1) == 1
            pick = (trait >> 1) & 3
            for h in range(pixels // HALF):
                totals = [None, None]
                for other in range(bands):
                    value = blocks_ref[rows, pl.ds(other * pixels + h * HALF, HALF)].astype(f32)
                    for plan in range(2):
                        band = pair_bands[plan]
                        own = 1.0 if band == other else 0.0
                        mix = jnp.where(
                            is_second,
                            own + offset_ref[1, band, other],
                            own + offset_ref[0, band, other],
                        )
                        term = mix * value
                        totals[plan] = term if other == 0 else totals[plan] + term
                for plan in range(2):
                    for k in range(picks):
                        spread[plan, rows, pl.ds(k * pixels + h * HALF, HALF)] = jnp.where(
                            pick == k, totals[plan], 0.0
                        ).astype(bf16)

        for plan in range(2):
            band = pair_bands[plan]
            resampled = jnp.dot(
                spread[plan], weights_ref[...], preferred_element_type=f32
            ).astype(bf16)
            moved = jnp.dot(choose_out[plan], resampled, preferred_element_type=f32)
            outgoing[band] = moved.astype(bf16).reshape(PEERS, SLOTS, pixels)
            incoming[band, 0] = outgoing[band, 0]

        if first_band == 0:
            pl.semaphore_wait(beside_sem, 7)

        @pl.loop(1, PEERS)
        def _(t):
            for plan in range(2):
                band = pair_bands[plan]
                pltpu.make_async_remote_copy(
                    src_ref=outgoing.at[band, t],
                    dst_ref=incoming.at[band, t],
                    send_sem=send_sem.at[band],
                    recv_sem=recv_sem.at[band],
                    device_id=peer(plan, t),
                    device_id_type=MESH,
                ).start()

        if first_band == 0:
            for plan in range(2):
                to_peer = (lax.broadcasted_iota(i32, (PEERS, blocks), 0) == numbers[plan]).astype(f32).astype(bf16)
                lane_slot = lax.broadcasted_iota(i32, (128, blocks), 0) & (SLOTS - 1)
                marks = jnp.where(lane_slot == slots[plan], cell_ref[...] + 1, 0).astype(f32).astype(bf16)
                found = lax.dot_general(
                    to_peer, marks, (((1,), (1,)), ((), ())), preferred_element_type=f32
                )
                lane = lax.broadcasted_iota(i32, (PEERS, 128), 1) & (SLOTS - 1)
                base = ((lane >> 1) * cells - 1).astype(f32)
                tags_out[plan] = jnp.where(found > 0.0, base + found, -1.0).reshape(PEERS, 1, 128)
                tags_in[plan, 0] = tags_out[plan, 0]

            @pl.loop(1, PEERS)
            def _(t):
                for plan in range(2):
                    pltpu.make_async_remote_copy(
                        src_ref=tags_out.at[plan, t],
                        dst_ref=tags_in.at[plan, t],
                        send_sem=tag_send_sem.at[plan],
                        recv_sem=tag_recv_sem.at[plan],
                        device_id=peer(plan, t),
                        device_id_type=MESH,
                    ).start()

    rest = pl.ds(1, PEERS - 1)
    sublane = lax.broadcasted_iota(i32, (8, 128), 0)
    lane_group = lax.broadcasted_iota(i32, (8, 128), 1) >> 4
    line = lax.broadcasted_iota(i32, (RING * cells, 128), 0).astype(f32)
    for plan in range(2):
        pltpu.make_async_copy(
            tags_in.at[plan, rest], tags_in.at[plan, rest], tag_recv_sem.at[plan]
        ).wait()
        arrived = tags_in[plan].reshape(PEERS, 128)
        for g in range(PEERS // 8):
            code = jnp.sum(
                jnp.where(sublane == lane_group, arrived[g * 8 : (g + 1) * 8], 0.0),
                axis=0,
                keepdims=True,
            )
            choose_in[plan, :, pl.ds(g * 128, 128)] = (line == code).astype(f32).astype(bf16)

    def gather_pair(plan, pair):
        for band in (plan * 4 + pair * 2, plan * 4 + pair * 2 + 1):
            pltpu.make_async_copy(
                incoming.at[band, rest], incoming.at[band, rest], recv_sem.at[band]
            ).wait()
            sums[band] = jnp.dot(
                choose_in[plan],
                incoming[band].reshape(PEERS * SLOTS, pixels),
                preferred_element_type=f32,
            )

    def ring_copy(plan, pair, sign, step):
        stream = STREAMS.index((plan, pair, sign))
        if plan == 0:
            device = (tile, (row + sign + 8) % 8)
        else:
            device = (((z + sign + 8) % 8) * 8 + x * 2 + core, row)
        return pltpu.make_async_remote_copy(
            src_ref=ring_out.at[stream, step],
            dst_ref=ring_in.at[stream, step],
            send_sem=ring_send_sem.at[stream, step],
            recv_sem=ring_recv_sem.at[stream, step],
            device_id=device,
            device_id_type=MESH,
        )

    def ring_step(pair, step):
        for plan in range(2):
            if step == 0:
                gather_pair(plan, pair)
            for sign in (1, -1):
                length = hops(pair, sign)
                if step >= length:
                    continue
                stream = STREAMS.index((plan, pair, sign))
                toward = (place[plan] + sign * (length - step) + 8) % 8
                lines = pl.ds(pl.multiple_of(toward * cells, cells), cells)
                if step > 0:
                    ring_copy(plan, pair, sign, step - 1).wait_recv()
                for i in range(2):
                    value = sums[plan * 4 + pair * 2 + i, lines, :]
                    if step > 0:
                        value = value + ring_in[stream, step - 1, i].astype(f32)
                    ring_out[stream, step, i] = value.astype(bf16)
                ring_copy(plan, pair, sign, step).start()

    def finish(pair):
        for plan in range(2):
            lines = pl.ds(pl.multiple_of(place[plan] * cells, cells), cells)
            for sign in (1, -1):
                ring_copy(plan, pair, sign, hops(pair, sign) - 1).wait_recv()
            for i in range(2):
                band = plan * 4 + pair * 2 + i
                total = sums[band, lines, :]
                for sign in (1, -1):
                    stream = STREAMS.index((plan, pair, sign))
                    total = total + ring_in[stream, hops(pair, sign) - 1, i].astype(f32)
                grid[pl.ds(8, cells), pl.ds(band * pixels, pixels)] = total

    span = 2 * pixels

    def edge_copy(pair, side):
        return pltpu.make_async_remote_copy(
            src_ref=edge_out.at[pair, side],
            dst_ref=edge_in.at[pair, side],
            send_sem=edge_send_sem.at[pair, side],
            recv_sem=edge_recv_sem.at[pair, side],
            device_id=(tile, (row + (1, 7)[side]) % 8),
            device_id_type=MESH,
        )

    def send_edges(pair):
        for side, line_at in ((0, 8 + cells - 1), (1, 8)):
            for plan in range(2):
                edge_out[pair, side, :, pl.ds(plan * span, span)] = grid[
                    pl.ds(line_at, 1), pl.ds((plan * 2 + pair) * span, span)
                ]
            edge_copy(pair, side).start()

    def smooth(pair):
        for side in range(2):
            edge_copy(pair, side).wait()
        for plan in range(2):
            lanes = pl.ds((plan * 2 + pair) * span, span)
            held = pl.ds(plan * span, span)
            grid[pl.ds(7, 1), lanes] = jnp.where(row == 0, 0.0, edge_in[pair, 0, :, held])
            grid[pl.ds(8 + cells, 1), lanes] = jnp.where(row == 7, 0.0, edge_in[pair, 1, :, held])
            for g in range(cells // 16):
                above = grid[pl.ds(g * 16 + 7, 16), lanes]
                here = grid[pl.ds(g * 16 + 8, 16), lanes]
                below = grid[pl.ds(g * 16 + 9, 16), lanes]
                smoothed = 0.25 * above + 0.5 * here + 0.25 * below
                rows = pl.ds(g * 16, 16)
                out_ref[rows, lanes] = (smoothed * factor[rows, lanes]).astype(bf16)

    ring_step(0, 0)

    for load in loads[2:]:
        load.wait()
    bins = table_ref.shape[1] - 1

    @pl.loop(0, cells // 8)
    def _(g):
        rows = pl.ds(pl.multiple_of(g * 8, 8), 8)
        which = bin_ref[rows, :]
        part = frac_ref[rows, :]
        volume_angle = vol_ref[rows, :]
        geometric_angle = geo_ref[rows, :]
        keep = mask_ref[rows, :].astype(f32)
        lower = [jnp.full((8, pixels), table_ref[b, 0]) for b in range(bands)]
        upper = [jnp.full((8, pixels), table_ref[b, 1]) for b in range(bands)]
        for n in range(1, bins):
            here = which == n
            for b in range(bands):
                lower[b] = jnp.where(here, table_ref[b, n], lower[b])
                upper[b] = jnp.where(here, table_ref[b, n + 1], upper[b])
        for b in range(bands):
            value = lower[b] * (1.0 - part) + upper[b] * part
            isotropic, volume, geometric = brdf_ref[0, b], brdf_ref[1, b], brdf_ref[2, b]
            numerator = isotropic + volume * nadir_volume + geometric * nadir_geometric
            denominator = isotropic + volume * volume_angle + geometric * geometric_angle
            factor[rows, pl.ds(b * pixels, pixels)] = value * (numerator / denominator) * keep

    ring_step(0, 1)
    ring_step(1, 0)
    ring_step(0, 2)
    ring_step(1, 1)
    ring_step(0, 3)
    ring_step(1, 2)
    finish(0)
    send_edges(0)
    ring_step(1, 3)
    smooth(0)
    finish(1)
    send_edges(1)
    for plan in range(2):
        pltpu.make_async_copy(
            tags_out.at[plan, rest], tags_out.at[plan, rest], tag_send_sem.at[plan]
        ).wait()
    for band in range(bands):
        pltpu.make_async_copy(
            outgoing.at[band, rest], outgoing.at[band, rest], send_sem.at[band]
        ).wait()
    for plan, pair, sign in STREAMS:
        for step in range(hops(pair, sign)):
            ring_copy(plan, pair, sign, step).wait_send()
    smooth(1)


def on_device(
    swath_blocks,
    footprint,
    cell_row,
    tile_pick,
    sensor,
    bandpass_offset,
    weight_tiles,
    lookup_table,
    lookup_bin,
    lookup_frac,
    brdf_params,
    vol_kernel,
    geo_kernel,
    clear_mask,
):
    blocks = swath_blocks.shape[2]
    width = swath_blocks.shape[3]
    bands = bandpass_offset.shape[1]
    pixels = width // bands
    picks = weight_tiles.shape[0]
    cells = lookup_bin.shape[1]
    smem = pl.BlockSpec(memory_space=pltpu.SMEM)
    vmem = pl.BlockSpec(memory_space=pltpu.VMEM)
    hbm = pl.BlockSpec(memory_space=pl.ANY)
    f32, bf16 = jnp.float32, jnp.bfloat16
    dma = pltpu.SemaphoreType.DMA
    result = pl.pallas_call(
        kernel,
        out_shape=jax.ShapeDtypeStruct((cells, width), bf16),
        in_specs=[smem] * 3 + [hbm] + [vmem] * 4 + [hbm] * 6,
        out_specs=vmem,
        scratch_shapes=[
            pltpu.VMEM((blocks, width), bf16),
            pltpu.VMEM((picks * pixels, pixels), bf16),
            pltpu.VMEM((cells, pixels), jnp.int32),
            pltpu.VMEM((cells, pixels), f32),
            pltpu.VMEM((cells, pixels), f32),
            pltpu.VMEM((cells, pixels), f32),
            pltpu.VMEM((cells, pixels), jnp.int32),
            pltpu.VMEM((blocks, 128), jnp.int32),
            pltpu.VMEM((2, blocks, picks * pixels), bf16),
            pltpu.VMEM((2, PEERS * SLOTS, blocks), bf16),
            pltpu.VMEM((2, RING * cells, PEERS * SLOTS), bf16),
            pltpu.VMEM((bands, PEERS, SLOTS, pixels), bf16),
            pltpu.VMEM((bands, PEERS, SLOTS, pixels), bf16),
            pltpu.VMEM((2, PEERS, 1, 128), f32),
            pltpu.VMEM((2, PEERS, 1, 128), f32),
            pltpu.VMEM((bands, RING * cells, pixels), f32),
            pltpu.VMEM((len(STREAMS), 4, 2, cells, pixels), bf16),
            pltpu.VMEM((len(STREAMS), 4, 2, cells, pixels), bf16),
            pltpu.VMEM((cells + 16, width), f32),
            pltpu.VMEM((cells, width), f32),
            pltpu.VMEM((2, 2, 1, width // 2), f32),
            pltpu.VMEM((2, 2, 1, width // 2), f32),
            dma((bands,)),
            dma((bands,)),
            dma((2,)),
            dma((2,)),
            dma((len(STREAMS), 4)),
            dma((len(STREAMS), 4)),
            dma((2, 2)),
            dma((2, 2)),
            pltpu.SemaphoreType.REGULAR,
            dma((7,)),
        ],
        compiler_params=pltpu.CompilerParams(
            has_side_effects=True, collective_id=0, vmem_limit_bytes=58 * 1024 * 1024
        ),
    )(
        bandpass_offset,
        lookup_table,
        brdf_params.T,
        swath_blocks.reshape(blocks, width),
        footprint.reshape(1, blocks),
        cell_row.reshape(1, blocks),
        tile_pick.reshape(1, blocks),
        sensor.reshape(1, blocks),
        weight_tiles.reshape(picks * pixels, pixels),
        lookup_bin[0],
        lookup_frac[0],
        vol_kernel[0],
        geo_kernel[0],
        clear_mask[0],
    )
    return result[None]


def solution(mesh):
    in_specs = (
        P("tile", "row", None, None),
        P("tile", "row", None, None),
        P("tile", "row", None),
        P("tile", "row", None),
        P("tile", "row", None),
        P(),
        P(),
        P(),
        P("tile", "row", None),
        P("tile", "row", None),
        P(),
        P("tile", "row", None),
        P("tile", "row", None),
        P("tile", "row", None),
    )
    return jax.shard_map(
        on_device, mesh=mesh, in_specs=in_specs, out_specs=P("tile", "row", None), check_vma=False
    )
```

```python
import jax
import jax.numpy as jnp
from jax import lax
from jax.experimental import pallas as pl
from jax.experimental.pallas import tpu as pltpu
from jax.sharding import PartitionSpec as P

nadir_volume = 0.3
nadir_geometric = 0.6
MESH = pl.DeviceIdType.MESH
RING = 8
PEERS = 64
SLOTS = 16
HALF = 128
STREAMS = [(plan, pair, sign) for pair in range(2) for plan in range(2) for sign in (1, -1)]


def hops(pair, sign):
    return 4 if (pair == 0) == (sign > 0) else 3


def kernel(
    offset_ref,
    table_ref,
    brdf_ref,
    blocks_hbm,
    target_ref,
    cell_ref,
    pick_ref,
    sensor_ref,
    weights_hbm,
    bin_hbm,
    frac_hbm,
    vol_hbm,
    geo_hbm,
    mask_hbm,
    out_ref,
    blocks_ref,
    weights_ref,
    bin_ref,
    frac_ref,
    vol_ref,
    geo_ref,
    mask_ref,
    traits,
    spread,
    choose_out,
    choose_in,
    outgoing,
    incoming,
    tags_out,
    tags_in,
    sums,
    ring_out,
    ring_in,
    grid,
    factor,
    edge_out,
    edge_in,
    send_sem,
    recv_sem,
    tag_send_sem,
    tag_recv_sem,
    ring_send_sem,
    ring_recv_sem,
    edge_send_sem,
    edge_recv_sem,
    beside_sem,
    load_sem,
):
    blocks = blocks_ref.shape[0]
    bands = 8
    pixels = 256
    cells = out_ref.shape[0]
    picks = weights_ref.shape[0] // pixels
    f32, bf16, i32 = jnp.float32, jnp.bfloat16, jnp.int32
    tile = lax.axis_index("tile")
    row = lax.axis_index("row")
    z, x, core = tile // 8, (tile // 2) % 4, tile % 2
    place = (row, z)

    def peer(plan, t):
        step = t % RING
        other = (t // RING + t) % RING
        side = ((x + other // 2) % 4) * 2 + (core + other % 2) % 2
        if plan == 0:
            return ((z + step) % 8) * 8 + side, row
        return z * 8 + side, (row + step) % 8

    around = pltpu.get_barrier_semaphore()
    for step in range(1, 8):
        side = ((x + step // 2) % 4) * 2 + (core + step % 2) % 2
        for device in (
            (((z + step) % 8) * 8 + x * 2 + core, row),
            (tile, (row + step) % 8),
            (z * 8 + side, row),
        ):
            pl.semaphore_signal(around, inc=1, device_id=device, device_id_type=MESH)
    loads = [
        pltpu.make_async_copy(source, kept, load_sem.at[i])
        for i, (source, kept) in enumerate(
            (
                (blocks_hbm, blocks_ref),
                (weights_hbm, weights_ref),
                (bin_hbm, bin_ref),
                (frac_hbm, frac_ref),
                (vol_hbm, vol_ref),
                (geo_hbm, geo_ref),
                (mask_hbm, mask_ref),
            )
        )
    ]
    for load in loads:
        load.start()

    target = target_ref[...]
    joined = ((target * 8 + pick_ref[...] * 2 + sensor_ref[...])).astype(f32)
    for j in range(blocks // 128):
        part = jnp.broadcast_to(joined[:, j * 128 : (j + 1) * 128], (128, 128))
        traits[pl.ds(j * 128, 128), :] = jnp.transpose(part).astype(i32)
    rank_parts = []
    own_target = traits[...] >> 3
    first = lax.broadcasted_iota(i32, (blocks, 128), 0)
    for j in range(blocks // 128):
        second = lax.broadcasted_iota(i32, (blocks, 128), 1) + j * 128
        same = (own_target == target[:, j * 128 : (j + 1) * 128]) & (first < second)
        rank_parts.append(jnp.sum(same.astype(f32), axis=0, keepdims=True))
    rank = jnp.concatenate(rank_parts, axis=1).astype(i32)

    to_row = target & 7
    to_z = target >> 6
    to_x = (target >> 4) & 3
    to_core = (target >> 3) & 1
    other = ((to_x - x) & 3) * 2 + ((to_core - core) & 1)
    numbers, slots = [], []
    for plan in range(2):
        step = ((to_z - z) & 7) if plan == 0 else ((to_row - row) & 7)
        number = ((other - step) & 7) * 8 + step
        slot = (to_row if plan == 0 else to_z) * 2 + rank
        position = number * SLOTS + slot
        for i in range(PEERS * SLOTS // 128):
            here = lax.broadcasted_iota(i32, (128, blocks), 0) + i * 128
            choose_out[plan, pl.ds(i * 128, 128), :] = (position == here).astype(f32).astype(bf16)
        numbers.append(number)
        slots.append(slot)

    pl.semaphore_wait(around, 21)
    for step in range(1, 8):
        side = ((x + step // 2) % 4) * 2 + (core + step % 2) % 2
        pl.semaphore_signal(
            beside_sem, inc=1, device_id=(z * 8 + side, row), device_id_type=MESH
        )

    loads[0].wait()
    loads[1].wait()
    for first_band in range(4):
        pair_bands = (first_band, first_band + 4)

        @pl.loop(0, blocks // 64)
        def _(g):
            rows = pl.ds(pl.multiple_of(g * 64, 64), 64)
            trait = traits[rows, :]
            is_second = (trait & 1) == 1
            pick = (trait >> 1) & 3
            for h in range(pixels // HALF):
                totals = [None, None]
                for other in range(bands):
                    value = blocks_ref[rows, pl.ds(other * pixels + h * HALF, HALF)].astype(f32)
                    for plan in range(2):
                        band = pair_bands[plan]
                        own = 1.0 if band == other else 0.0
                        mix = jnp.where(
                            is_second,
                            own + offset_ref[1, band, other],
                            own + offset_ref[0, band, other],
                        )
                        term = mix * value
                        totals[plan] = term if other == 0 else totals[plan] + term
                for plan in range(2):
                    for k in range(picks):
                        spread[plan, rows, pl.ds(k * pixels + h * HALF, HALF)] = jnp.where(
                            pick == k, totals[plan], 0.0
                        ).astype(bf16)

        for plan in range(2):
            band = pair_bands[plan]
            resampled = jnp.dot(
                spread[plan], weights_ref[...], preferred_element_type=f32
            ).astype(bf16)
            moved = jnp.dot(choose_out[plan], resampled, preferred_element_type=f32)
            outgoing[band] = moved.astype(bf16).reshape(PEERS, SLOTS, pixels)
            incoming[band, 0] = outgoing[band, 0]

        if first_band == 0:
            pl.semaphore_wait(beside_sem, 7)

        @pl.loop(1, PEERS)
        def _(t):
            for plan in range(2):
                band = pair_bands[plan]
                pltpu.make_async_remote_copy(
                    src_ref=outgoing.at[band, t],
                    dst_ref=incoming.at[band, t],
                    send_sem=send_sem.at[band],
                    recv_sem=recv_sem.at[band],
                    device_id=peer(plan, t),
                    device_id_type=MESH,
                ).start()

        if first_band == 2:
            for plan in range(2):
                to_peer = (lax.broadcasted_iota(i32, (PEERS, blocks), 0) == numbers[plan]).astype(f32).astype(bf16)
                lane_slot = lax.broadcasted_iota(i32, (128, blocks), 0) & (SLOTS - 1)
                marks = jnp.where(lane_slot == slots[plan], cell_ref[...] + 1, 0).astype(f32).astype(bf16)
                found = lax.dot_general(
                    to_peer, marks, (((1,), (1,)), ((), ())), preferred_element_type=f32
                )
                lane = lax.broadcasted_iota(i32, (PEERS, 128), 1) & (SLOTS - 1)
                base = ((lane >> 1) * cells - 1).astype(f32)
                tags_out[plan] = jnp.where(found > 0.0, base + found, -1.0).reshape(PEERS, 1, 128)
                tags_in[plan, 0] = tags_out[plan, 0]

            @pl.loop(1, PEERS)
            def _(t):
                for plan in range(2):
                    pltpu.make_async_remote_copy(
                        src_ref=tags_out.at[plan, t],
                        dst_ref=tags_in.at[plan, t],
                        send_sem=tag_send_sem.at[plan],
                        recv_sem=tag_recv_sem.at[plan],
                        device_id=peer(plan, t),
                        device_id_type=MESH,
                    ).start()

    rest = pl.ds(1, PEERS - 1)
    sublane = lax.broadcasted_iota(i32, (8, 128), 0)
    lane_group = lax.broadcasted_iota(i32, (8, 128), 1) >> 4
    line = lax.broadcasted_iota(i32, (RING * cells, 128), 0).astype(f32)
    for plan in range(2):
        pltpu.make_async_copy(
            tags_in.at[plan, rest], tags_in.at[plan, rest], tag_recv_sem.at[plan]
        ).wait()
        arrived = tags_in[plan].reshape(PEERS, 128)
        for g in range(PEERS // 8):
            code = jnp.sum(
                jnp.where(sublane == lane_group, arrived[g * 8 : (g + 1) * 8], 0.0),
                axis=0,
                keepdims=True,
            )
            choose_in[plan, :, pl.ds(g * 128, 128)] = (line == code).astype(f32).astype(bf16)

    def gather_pair(plan, pair):
        for band in (plan * 4 + pair * 2, plan * 4 + pair * 2 + 1):
            pltpu.make_async_copy(
                incoming.at[band, rest], incoming.at[band, rest], recv_sem.at[band]
            ).wait()
            sums[band] = jnp.dot(
                choose_in[plan],
                incoming[band].reshape(PEERS * SLOTS, pixels),
                preferred_element_type=f32,
            )

    def ring_copy(plan, pair, sign, step):
        stream = STREAMS.index((plan, pair, sign))
        if plan == 0:
            device = (tile, (row + sign + 8) % 8)
        else:
            device = (((z + sign + 8) % 8) * 8 + x * 2 + core, row)
        return pltpu.make_async_remote_copy(
            src_ref=ring_out.at[stream, step],
            dst_ref=ring_in.at[stream, step],
            send_sem=ring_send_sem.at[stream, step],
            recv_sem=ring_recv_sem.at[stream, step],
            device_id=device,
            device_id_type=MESH,
        )

    def ring_step(pair, step):
        for plan in range(2):
            if step == 0:
                gather_pair(plan, pair)
            for sign in (1, -1):
                length = hops(pair, sign)
                if step >= length:
                    continue
                stream = STREAMS.index((plan, pair, sign))
                toward = (place[plan] + sign * (length - step) + 8) % 8
                lines = pl.ds(pl.multiple_of(toward * cells, cells), cells)
                if step > 0:
                    ring_copy(plan, pair, sign, step - 1).wait_recv()
                for i in range(2):
                    value = sums[plan * 4 + pair * 2 + i, lines, :]
                    if step > 0:
                        value = value + ring_in[stream, step - 1, i].astype(f32)
                    ring_out[stream, step, i] = value.astype(bf16)
                ring_copy(plan, pair, sign, step).start()

    def finish(pair):
        for plan in range(2):
            lines = pl.ds(pl.multiple_of(place[plan] * cells, cells), cells)
            for sign in (1, -1):
                ring_copy(plan, pair, sign, hops(pair, sign) - 1).wait_recv()
            for i in range(2):
                band = plan * 4 + pair * 2 + i
                total = sums[band, lines, :]
                for sign in (1, -1):
                    stream = STREAMS.index((plan, pair, sign))
                    total = total + ring_in[stream, hops(pair, sign) - 1, i].astype(f32)
                grid[pl.ds(8, cells), pl.ds(band * pixels, pixels)] = total

    span = 2 * pixels

    def edge_copy(pair, side):
        return pltpu.make_async_remote_copy(
            src_ref=edge_out.at[pair, side],
            dst_ref=edge_in.at[pair, side],
            send_sem=edge_send_sem.at[pair, side],
            recv_sem=edge_recv_sem.at[pair, side],
            device_id=(tile, (row + (1, 7)[side]) % 8),
            device_id_type=MESH,
        )

    def send_edges(pair):
        for side, line_at in ((0, 8 + cells - 1), (1, 8)):
            for plan in range(2):
                edge_out[pair, side, :, pl.ds(plan * span, span)] = grid[
                    pl.ds(line_at, 1), pl.ds((plan * 2 + pair) * span, span)
                ]
            edge_copy(pair, side).start()

    def smooth(pair):
        for side in range(2):
            edge_copy(pair, side).wait()
        for plan in range(2):
            lanes = pl.ds((plan * 2 + pair) * span, span)
            held = pl.ds(plan * span, span)
            grid[pl.ds(7, 1), lanes] = jnp.where(row == 0, 0.0, edge_in[pair, 0, :, held])
            grid[pl.ds(8 + cells, 1), lanes] = jnp.where(row == 7, 0.0, edge_in[pair, 1, :, held])
            for g in range(cells // 16):
                above = grid[pl.ds(g * 16 + 7, 16), lanes]
                here = grid[pl.ds(g * 16 + 8, 16), lanes]
                below = grid[pl.ds(g * 16 + 9, 16), lanes]
                smoothed = 0.25 * above + 0.5 * here + 0.25 * below
                rows = pl.ds(g * 16, 16)
                out_ref[rows, lanes] = (smoothed * factor[rows, lanes]).astype(bf16)

    ring_step(0, 0)

    for load in loads[2:]:
        load.wait()
    bins = table_ref.shape[1] - 1

    @pl.loop(0, cells // 8)
    def _(g):
        rows = pl.ds(pl.multiple_of(g * 8, 8), 8)
        which = bin_ref[rows, :]
        part = frac_ref[rows, :]
        volume_angle = vol_ref[rows, :]
        geometric_angle = geo_ref[rows, :]
        keep = mask_ref[rows, :].astype(f32)
        lower = [jnp.full((8, pixels), table_ref[b, 0]) for b in range(bands)]
        upper = [jnp.full((8, pixels), table_ref[b, 1]) for b in range(bands)]
        for n in range(1, bins):
            here = which == n
            for b in range(bands):
                lower[b] = jnp.where(here, table_ref[b, n], lower[b])
                upper[b] = jnp.where(here, table_ref[b, n + 1], upper[b])
        for b in range(bands):
            value = lower[b] * (1.0 - part) + upper[b] * part
            isotropic, volume, geometric = brdf_ref[0, b], brdf_ref[1, b], brdf_ref[2, b]
            numerator = isotropic + volume * nadir_volume + geometric * nadir_geometric
            denominator = isotropic + volume * volume_angle + geometric * geometric_angle
            factor[rows, pl.ds(b * pixels, pixels)] = value * (numerator / denominator) * keep

    ring_step(0, 1)
    ring_step(1, 0)
    ring_step(0, 2)
    ring_step(1, 1)
    ring_step(0, 3)
    ring_step(1, 2)
    finish(0)
    send_edges(0)
    ring_step(1, 3)
    smooth(0)
    finish(1)
    send_edges(1)
    for plan in range(2):
        pltpu.make_async_copy(
            tags_out.at[plan, rest], tags_out.at[plan, rest], tag_send_sem.at[plan]
        ).wait()
    for band in range(bands):
        pltpu.make_async_copy(
            outgoing.at[band, rest], outgoing.at[band, rest], send_sem.at[band]
        ).wait()
    for plan, pair, sign in STREAMS:
        for step in range(hops(pair, sign)):
            ring_copy(plan, pair, sign, step).wait_send()
    smooth(1)


def on_device(
    swath_blocks,
    footprint,
    cell_row,
    tile_pick,
    sensor,
    bandpass_offset,
    weight_tiles,
    lookup_table,
    lookup_bin,
    lookup_frac,
    brdf_params,
    vol_kernel,
    geo_kernel,
    clear_mask,
):
    blocks = swath_blocks.shape[2]
    width = swath_blocks.shape[3]
    bands = bandpass_offset.shape[1]
    pixels = width // bands
    picks = weight_tiles.shape[0]
    cells = lookup_bin.shape[1]
    smem = pl.BlockSpec(memory_space=pltpu.SMEM)
    vmem = pl.BlockSpec(memory_space=pltpu.VMEM)
    hbm = pl.BlockSpec(memory_space=pl.ANY)
    f32, bf16 = jnp.float32, jnp.bfloat16
    dma = pltpu.SemaphoreType.DMA
    result = pl.pallas_call(
        kernel,
        out_shape=jax.ShapeDtypeStruct((cells, width), bf16),
        in_specs=[smem] * 3 + [hbm] + [vmem] * 4 + [hbm] * 6,
        out_specs=vmem,
        scratch_shapes=[
            pltpu.VMEM((blocks, width), bf16),
            pltpu.VMEM((picks * pixels, pixels), bf16),
            pltpu.VMEM((cells, pixels), jnp.int32),
            pltpu.VMEM((cells, pixels), f32),
            pltpu.VMEM((cells, pixels), f32),
            pltpu.VMEM((cells, pixels), f32),
            pltpu.VMEM((cells, pixels), jnp.int32),
            pltpu.VMEM((blocks, 128), jnp.int32),
            pltpu.VMEM((2, blocks, picks * pixels), bf16),
            pltpu.VMEM((2, PEERS * SLOTS, blocks), bf16),
            pltpu.VMEM((2, RING * cells, PEERS * SLOTS), bf16),
            pltpu.VMEM((bands, PEERS, SLOTS, pixels), bf16),
            pltpu.VMEM((bands, PEERS, SLOTS, pixels), bf16),
            pltpu.VMEM((2, PEERS, 1, 128), f32),
            pltpu.VMEM((2, PEERS, 1, 128), f32),
            pltpu.VMEM((bands, RING * cells, pixels), f32),
            pltpu.VMEM((len(STREAMS), 4, 2, cells, pixels), bf16),
            pltpu.VMEM((len(STREAMS), 4, 2, cells, pixels), bf16),
            pltpu.VMEM((cells + 16, width), f32),
            pltpu.VMEM((cells, width), f32),
            pltpu.VMEM((2, 2, 1, width // 2), f32),
            pltpu.VMEM((2, 2, 1, width // 2), f32),
            dma((bands,)),
            dma((bands,)),
            dma((2,)),
            dma((2,)),
            dma((len(STREAMS), 4)),
            dma((len(STREAMS), 4)),
            dma((2, 2)),
            dma((2, 2)),
            pltpu.SemaphoreType.REGULAR,
            dma((7,)),
        ],
        compiler_params=pltpu.CompilerParams(
            has_side_effects=True, collective_id=0, vmem_limit_bytes=58 * 1024 * 1024
        ),
    )(
        bandpass_offset,
        lookup_table,
        brdf_params.T,
        swath_blocks.reshape(blocks, width),
        footprint.reshape(1, blocks),
        cell_row.reshape(1, blocks),
        tile_pick.reshape(1, blocks),
        sensor.reshape(1, blocks),
        weight_tiles.reshape(picks * pixels, pixels),
        lookup_bin[0],
        lookup_frac[0],
        vol_kernel[0],
        geo_kernel[0],
        clear_mask[0],
    )
    return result[None]


def solution(mesh):
    in_specs = (
        P("tile", "row", None, None),
        P("tile", "row", None, None),
        P("tile", "row", None),
        P("tile", "row", None),
        P("tile", "row", None),
        P(),
        P(),
        P(),
        P("tile", "row", None),
        P("tile", "row", None),
        P(),
        P("tile", "row", None),
        P("tile", "row", None),
        P("tile", "row", None),
    )
    return jax.shard_map(
        on_device, mesh=mesh, in_specs=in_specs, out_specs=P("tile", "row", None), check_vma=False
    )
```
